32 devices in a mesh: grp: 4 (over x, core), seq: 8 (over z, y).
Axes of the slice: x: 2, y: 2, z: 4, core: 2. Of those that a mesh axis runs over, the one named last changes fastest.
Arguments:
- cand_queries: bfloat16 [4096, 128, 128], P(('grp', 'seq')), may hold values from -256 to 256
- candidate_keys: bfloat16 [512, 128, 128], P(('grp', 'seq')), may hold values from -6 to 6
- candidate_values: bfloat16 [512, 128, 128], P(('grp', 'seq')), may hold values from -24 to 24
- prefix_rotated_keys: bfloat16 [128, 1024], P(('grp', 'seq')), may hold values from -6.1 to 6.1
- prefix_value_matrix: bfloat16 [128, 1024], P(('grp', 'seq')), may hold values from -24 to 24
- lengths: int32 [64], replicated, may hold values from 32 to 128
Outputs:
- attended: bfloat16 [4096, 128, 128], P(('grp', 'seq'))
The draws below stay inside these ranges and needn't reach their ends.
All inputs are finite; a program needn't handle non-finite values.
Results may differ from the reference program's by a relative error of at most 0.0076.
Values may be sent and summed in bfloat16 or wider, within the bound.
No kernel may reach another device: no remote copies, remote signals or barrier semaphores. Data moves between devices by JAX's collectives and lax.ppermute only.
A program may use at most 64 MiB of HBM per device.

```python
import math
import jax
import jax.numpy as jnp
from jax import lax

QUERY_HEADS = 64
KEY_VALUE_HEADS = 8
HEAD_WIDTH = 128
CANDIDATE_SLOTS = 128
CANDIDATE_TOTAL = 64
PREFIX_TOKENS = 128


def prefix_anchor(key):
    drawn_row_list = jax.random.normal(jax.random.fold_in(key, 11), (PREFIX_TOKENS, KEY_VALUE_HEADS, HEAD_WIDTH), jnp.float32)
    return jnp.clip(drawn_row_list, -6.0, 6.0)


def draw_prefix_rotated_keys(key, part):
    anchor_row_list = prefix_anchor(key)
    return anchor_row_list.reshape(PREFIX_TOKENS, KEY_VALUE_HEADS * HEAD_WIDTH).astype(jnp.bfloat16)


def draw_cand_queries(key, part):

    def one_candidate(index):
        own_key = jax.random.fold_in(key, 100 + index)
        noise = 2.0 * jax.random.normal(jax.random.fold_in(own_key, 21), (QUERY_HEADS, CANDIDATE_SLOTS, HEAD_WIDTH), jnp.float32)
        noise = jnp.clip(noise, -12.0, 12.0)
        return noise
    rows = lax.map(one_candidate, jnp.arange(CANDIDATE_TOTAL))
    return rows.reshape(CANDIDATE_TOTAL * QUERY_HEADS, CANDIDATE_SLOTS, HEAD_WIDTH).astype(jnp.bfloat16)


def place_ends(entries, stream_key, least, high):
    longest = entries.shape.index(max(entries.shape))
    spots = []
    for shift in (0, 1):
        where = [jax.random.randint(jax.random.fold_in(stream_key, axis), (), 0, length) for axis, length in enumerate(entries.shape)]
        where[longest] = (where[longest] + shift) % entries.shape[longest]
        spots.append(tuple(where))
    return entries.at[spots[0]].set(least).at[spots[1]].set(high)


def block_scale(key, dims, pieces, low, high):
    level = 1.0
    for position, shards_of in pieces:
        draws = jax.random.uniform(jax.random.fold_in(jax.random.fold_in(key, 6), position), (shards_of,), jnp.float32, low / len(pieces), high / len(pieces))
        level = level * jnp.repeat(jnp.exp(draws), dims[position] // shards_of).reshape((-1,) + (1,) * (len(dims) - 1 - position))
    return level


def scatter_about(key, extent, deviation, most, cuts=(), held_as=jnp.bfloat16):
    values = deviation * jax.random.normal(key, extent, jnp.float32)
    if cuts:
        values = values * block_scale(key, extent, cuts, -0.22, 0.18)
    return jnp.clip(values, -most, most).astype(held_as)


def setup_inputs(seed: int = 0) -> dict:
    key_of = jax.random.split(jax.random.key(seed), 7)
    return {
        "cand_queries": draw_cand_queries(jax.random.fold_in(key_of[6], 71), 0),
        "candidate_keys": scatter_about(key_of[1], (CANDIDATE_TOTAL * KEY_VALUE_HEADS, CANDIDATE_SLOTS, HEAD_WIDTH), 1.0, 6.0, ((0, 32),)),
        "candidate_values": scatter_about(key_of[2], (CANDIDATE_TOTAL * KEY_VALUE_HEADS, CANDIDATE_SLOTS, HEAD_WIDTH), 4.0, 24.0, ((0, 32),)),
        "prefix_rotated_keys": draw_prefix_rotated_keys(jax.random.fold_in(key_of[6], 71), 0),
        "prefix_value_matrix": scatter_about(key_of[4], (PREFIX_TOKENS, KEY_VALUE_HEADS * HEAD_WIDTH), 4.0, 24.0, ((0, 32),)),
        "lengths": place_ends(jax.random.randint(key_of[5], (CANDIDATE_TOTAL,), CANDIDATE_SLOTS // 4, CANDIDATE_SLOTS + 1), jax.random.fold_in(key_of[5], 1), CANDIDATE_SLOTS // 4, CANDIDATE_SLOTS).astype(jnp.int32),
    }


rope_base = 500000.0

def rotate(vectors, positions):
    half_width = vectors.shape[-1] // 2
    exponents = jnp.arange(half_width, dtype=jnp.float32) * (2.0 / vectors.shape[-1])
    frequency = 1.0 / jnp.power(jnp.float32(rope_base), exponents)
    angles = positions.astype(jnp.float32)[:, None] * frequency[None, :]
    cosine = jnp.cos(angles)
    sine_table = jnp.sin(angles)
    lower_half = vectors[..., :half_width]
    upper_half = vectors[..., half_width:]
    return jnp.concatenate([lower_half * cosine - upper_half * sine_table, upper_half * cosine + lower_half * sine_table], axis=-1)

def reference(cand_queries, candidate_keys, candidate_values, prefix_rotated_keys, prefix_value_matrix, lengths):
    group_width = QUERY_HEADS // KEY_VALUE_HEADS
    score_scale = 1.0 / math.sqrt(HEAD_WIDTH)
    positions = PREFIX_TOKENS + jnp.arange(CANDIDATE_SLOTS, dtype=jnp.int32)
    token_index = jnp.arange(CANDIDATE_SLOTS, dtype=jnp.int32)
    allowed = jnp.concatenate([jnp.ones((CANDIDATE_SLOTS, PREFIX_TOKENS), dtype=bool), token_index[None, :] <= token_index[:, None]], axis=1)
    prefix_heads_keys = prefix_rotated_keys.reshape(PREFIX_TOKENS, KEY_VALUE_HEADS, HEAD_WIDTH).transpose(1, 0, 2)
    prefix_heads_values = prefix_value_matrix.reshape(PREFIX_TOKENS, KEY_VALUE_HEADS, HEAD_WIDTH).transpose(1, 0, 2)
    queries_all = cand_queries.reshape(CANDIDATE_TOTAL, QUERY_HEADS, CANDIDATE_SLOTS, HEAD_WIDTH)
    joined_keys = candidate_keys.reshape(CANDIDATE_TOTAL, KEY_VALUE_HEADS, CANDIDATE_SLOTS, HEAD_WIDTH)
    joined_values = candidate_values.reshape(CANDIDATE_TOTAL, KEY_VALUE_HEADS, CANDIDATE_SLOTS, HEAD_WIDTH)

    def one_candidate(candidate_parts):
        query_rows, new_keys, new_values, length = candidate_parts
        query_rows = rotate(query_rows.astype(jnp.float32), positions).astype(jnp.bfloat16)
        new_keys = rotate(new_keys.astype(jnp.float32), positions).astype(jnp.bfloat16)
        all_keys = jnp.concatenate([prefix_heads_keys, new_keys], axis=1)
        all_values = jnp.concatenate([prefix_heads_values, new_values], axis=1)
        grouped_rows = query_rows.reshape(KEY_VALUE_HEADS, group_width, CANDIDATE_SLOTS, HEAD_WIDTH)

        def one_head(head_parts):
            head_query, head_keys, head_values = head_parts
            scores = jnp.einsum('gtd,nd->gtn', head_query.astype(jnp.float32), head_keys.astype(jnp.float32)) * score_scale
            scores = jnp.where(allowed[None], scores, -jnp.inf)
            maxima = lax.optimization_barrier(jnp.max(scores, axis=-1, keepdims=True))
            exponent = jnp.exp(scores - maxima)
            totals = lax.optimization_barrier(jnp.sum(exponent, axis=-1, keepdims=True))
            weights = exponent.astype(jnp.bfloat16)
            weighted = jnp.einsum('gtn,nd->gtd', weights.astype(jnp.float32), head_values.astype(jnp.float32))
            return weighted / totals
        head_outputs = lax.map(one_head, (grouped_rows, all_keys, all_values))
        result = head_outputs.reshape(QUERY_HEADS, CANDIDATE_SLOTS, HEAD_WIDTH)
        visible = token_index < length
        return jnp.where(visible[None, :, None], result, jnp.float32(0.0)).astype(jnp.bfloat16)
    outputs = lax.map(one_candidate, (queries_all, joined_keys, joined_values, lengths))
    return outputs.reshape(CANDIDATE_TOTAL * QUERY_HEADS, CANDIDATE_SLOTS, HEAD_WIDTH)
```

```python
import functools
import math

import jax
import jax.numpy as jnp
import numpy as np
from jax import lax
from jax.experimental import pallas as pl
from jax.experimental.pallas import tpu as pltpu
from jax.sharding import PartitionSpec as P

QUERY_HEADS = 64
KEY_VALUE_HEADS = 8
HEAD_WIDTH = 128

rope_base = 500000.0
exp2_scale = math.log2(math.e) / math.sqrt(HEAD_WIDTH)


def rotation_tables(first, count):
    half_width = HEAD_WIDTH // 2
    exponents = jnp.arange(half_width, dtype=jnp.float32) * (2.0 / HEAD_WIDTH)
    frequency = 1.0 / jnp.power(jnp.float32(rope_base), exponents)
    positions = (first + jnp.arange(count, dtype=jnp.int32)).astype(jnp.float32)
    angles = positions[:, None] * frequency[None, :]
    cosine = jnp.cos(angles)
    sine = jnp.sin(angles)
    return jnp.concatenate([cosine, cosine], axis=1), jnp.concatenate([-sine, sine], axis=1)


def attend_kernel(
    first_row,
    live,
    queries,
    keys,
    values,
    prefix,
    cosine,
    sine,
    out,
    staged,
    sems,
    *,
    heads,
    tile,
):
    rows, tokens, width = keys.shape
    group = queries.shape[0] // rows
    prefix_rows = prefix.shape[0]
    value_base = heads * width
    column = lax.broadcasted_iota(jnp.int32, (tile, tokens), 1)
    token = lax.broadcasted_iota(jnp.int32, (tile, tokens), 0)
    out_token = lax.broadcasted_iota(jnp.int32, (tile, width), 0)

    def rotate(x, start):
        x = x.astype(jnp.float32)
        size = x.shape[-2]
        cos = cosine[start : start + size]
        sin = sine[start : start + size]
        return (x * cos + pltpu.roll(x, width // 2, x.ndim - 1) * sin).astype(jnp.bfloat16)

    def one_row(r, carry):
        head = lax.rem(r, heads)
        length = live[lax.div(first_row[0] + r, KEY_VALUE_HEADS)]
        key_column = pl.multiple_of(head * width, width)
        value_column = pl.multiple_of(value_base + head * width, width)
        all_keys = jnp.concatenate(
            [prefix[:, pl.ds(key_column, width)], rotate(keys[r], 0)], axis=0
        )
        all_values = jnp.concatenate([prefix[:, pl.ds(value_column, width)], values[r]], axis=0)
        all_values = jnp.concatenate([all_values, jnp.ones_like(all_values)], axis=1)
        slot = pl.ds(pl.multiple_of(r * group, group), group)
        for start in range(0, tokens, tile):
            piece = slice(start, start + tile)
            q = rotate(queries[slot, piece, :], start).reshape(group * tile, width)
            scores = lax.dot_general(
                q, all_keys, (((1,), (1,)), ((), ())), preferred_element_type=jnp.float32
            )
            allowed = (column <= token + start)[None]
            own = jnp.where(
                allowed, scores[:, prefix_rows:].reshape(group, tile, tokens), -jnp.inf
            ).reshape(group * tile, tokens)
            scores = jnp.concatenate([scores[:, :prefix_rows], own], axis=1)
            highest = jnp.max(scores, axis=-1, keepdims=True)
            weights = jnp.exp2((scores - highest) * exp2_scale).astype(jnp.bfloat16)
            summed = jnp.dot(weights, all_values, preferred_element_type=jnp.float32)
            attended = summed[:, :width] / summed[:, width:]
            visible = (out_token + start < length)[None]
            attended = jnp.where(visible, attended.reshape(group, tile, width), 0.0)
            staged[slot, piece, :] = attended.astype(jnp.bfloat16)
        pltpu.make_async_copy(staged.at[slot], out.at[slot], sems.at[r]).start()
        return carry

    lax.fori_loop(0, rows, one_row, 0)

    def finish(r, carry):
        slot = pl.ds(pl.multiple_of(r * group, group), group)
        pltpu.make_async_copy(staged.at[slot], out.at[slot], sems.at[r]).wait()
        return carry

    lax.fori_loop(0, rows, finish, 0)


def attend(first_row, lengths, queries, keys, values, prefix, cosine, sine, heads):
    rows = keys.shape[0]
    in_vmem = pl.BlockSpec(memory_space=pltpu.VMEM)
    in_smem = pl.BlockSpec(memory_space=pltpu.SMEM)
    return pl.pallas_call(
        functools.partial(attend_kernel, heads=heads, tile=min(64, keys.shape[1])),
        out_shape=jax.ShapeDtypeStruct(queries.shape, jnp.bfloat16),
        in_specs=[in_smem, in_smem] + [in_vmem] * 6,
        out_specs=pl.BlockSpec(memory_space=pl.ANY),
        scratch_shapes=[
            pltpu.VMEM(queries.shape, jnp.bfloat16),
            pltpu.SemaphoreType.DMA((rows,)),
        ],
        compiler_params=pltpu.CompilerParams(vmem_limit_bytes=40 << 20),
        name="attend",
    )(first_row, lengths, queries, keys, values, prefix, cosine, sine)


def shards(
    cand_queries,
    candidate_keys,
    candidate_values,
    prefix_rotated_keys,
    prefix_value_matrix,
    lengths,
):
    sequence_count = lax.axis_size("seq")
    grp_count = lax.axis_size("grp")
    key_value_rows, cand_length, _ = candidate_keys.shape
    heads = min(KEY_VALUE_HEADS, key_value_rows)
    prefix_here = prefix_rotated_keys.shape[0]
    prefix_total = prefix_here * sequence_count * grp_count
    wanted = (
        np.arange(sequence_count)[:, None] * key_value_rows + np.arange(heads)[None, :]
    ) % KEY_VALUE_HEADS

    def by_target(matrix):
        if (wanted == np.arange(KEY_VALUE_HEADS)[None, :]).all():
            return jnp.broadcast_to(matrix[None], (sequence_count,) + matrix.shape)
        split = matrix.reshape(prefix_here, KEY_VALUE_HEADS, HEAD_WIDTH)
        picked = jnp.take(split, wanted.reshape(-1), axis=1)
        return picked.reshape(prefix_here, sequence_count, heads * HEAD_WIDTH).transpose(1, 0, 2)

    outgoing = jnp.concatenate([by_target(prefix_rotated_keys), by_target(prefix_value_matrix)], axis=2)
    spread = lax.all_to_all(outgoing, "seq", split_axis=0, concat_axis=0, tiled=True)
    spread = spread.reshape(sequence_count * prefix_here, 2 * heads * HEAD_WIDTH)
    prefix = lax.all_gather(spread, "grp", axis=0, tiled=True)
    cosine, sine = rotation_tables(prefix_total, cand_length)
    place = lax.axis_index("grp") * sequence_count + lax.axis_index("seq")
    first_row = (place * key_value_rows).astype(jnp.int32).reshape(1)
    return attend(
        first_row,
        lengths,
        cand_queries,
        candidate_keys,
        candidate_values,
        prefix,
        cosine,
        sine,
        heads,
    )


def solution(mesh):
    return jax.shard_map(
        shards,
        mesh=mesh,
        in_specs=(
            P(("grp", "seq"), None, None),
            P(("grp", "seq"), None, None),
            P(("grp", "seq"), None, None),
            P(("grp", "seq"), None),
            P(("grp", "seq"), None),
            P(),
        ),
        out_specs=P(("grp", "seq"), None, None),
        check_vma=False,
    )
```

```python
import functools
import math

import jax
import jax.numpy as jnp
import numpy as np
from jax import lax
from jax.experimental import pallas as pl
from jax.experimental.pallas import tpu as pltpu
from jax.sharding import PartitionSpec as P

QUERY_HEADS = 64
KEY_VALUE_HEADS = 8
HEAD_WIDTH = 128

rope_base = 500000.0
exp2_scale = math.log2(math.e) / math.sqrt(HEAD_WIDTH)
score_chunk = 64
rotate_vmem = 51_000_000


def rotation_tables(first, count):
    half_width = HEAD_WIDTH // 2
    exponents = jnp.arange(half_width, dtype=jnp.float32) * (2.0 / HEAD_WIDTH)
    frequency = 1.0 / jnp.power(jnp.float32(rope_base), exponents)
    positions = (first + jnp.arange(count, dtype=jnp.int32)).astype(jnp.float32)
    angles = positions[:, None] * frequency[None, :]
    cosine = jnp.cos(angles)
    sine = jnp.sin(angles)
    return jnp.concatenate([cosine, cosine], axis=1), jnp.concatenate([-sine, sine], axis=1)


def rows_of(index, count):
    return pl.ds(pl.multiple_of(index * count, count), count)


def rotate_kernel(cosine, sine, queries, keys, out_q, out_k, raw_q, raw_k, q_sems, key_sem):
    rows, tokens, width = keys.shape
    group = queries.shape[0] // rows

    def load(r):
        span = rows_of(r, group)
        return pltpu.make_async_copy(queries.at[span], raw_q.at[span], q_sems.at[r])

    keys_in = pltpu.make_async_copy(keys, raw_k, key_sem)

    def start(r, carry):
        load(r).start()
        return carry

    lax.fori_loop(0, rows, start, 0)
    keys_in.start()

    def rotate(x):
        x = x.astype(jnp.float32)
        turned = pltpu.roll(x, width // 2, x.ndim - 1)
        return (x * cosine[...] + turned * sine[...]).astype(jnp.bfloat16)

    def one_row(r, carry):
        load(r).wait()
        span = rows_of(r, group)
        out_q[span] = rotate(raw_q[span])
        return carry

    lax.fori_loop(0, rows, one_row, 0)
    keys_in.wait()

    def one_key_row(r, carry):
        out_k[r] = rotate(raw_k[r])
        return carry

    lax.fori_loop(0, rows, one_key_row, 0)


def rotated(cosine, sine, queries, keys):
    rows = keys.shape[0]
    in_vmem = pl.BlockSpec(memory_space=pltpu.VMEM)
    in_hbm = pl.BlockSpec(memory_space=pltpu.HBM)
    shape = lambda x: jax.ShapeDtypeStruct(x.shape, jnp.bfloat16)
    return pl.pallas_call(
        rotate_kernel,
        out_shape=[shape(queries), shape(keys)],
        in_specs=[in_vmem] * 2 + [in_hbm] * 2,
        out_specs=[in_vmem] * 2,
        scratch_shapes=[
            pltpu.VMEM(queries.shape, jnp.bfloat16),
            pltpu.VMEM(keys.shape, jnp.bfloat16),
            pltpu.SemaphoreType.DMA((rows,)),
            pltpu.SemaphoreType.DMA(()),
        ],
        cost_estimate=pl.CostEstimate(
            flops=6 * queries.size, bytes_accessed=2 * queries.size, transcendentals=0
        ),
        compiler_params=pltpu.CompilerParams(vmem_limit_bytes=rotate_vmem),
        name="rotate",
    )(cosine, sine, queries, keys)


def attend_kernel(live, queries, keys, values, prefix, out, staged, *scratch, heads, block, tile):
    score_slots, weight_slots, sems = scratch[:2], scratch[2:4], scratch[4]
    rows, tokens, width = keys.shape
    group = queries.shape[0] // rows
    prefix_rows = prefix.shape[0]
    value_base = heads * width
    place = lax.axis_index("grp") * lax.axis_size("seq") + lax.axis_index("seq")
    column = lax.broadcasted_iota(jnp.int32, (tile, tokens), 1)
    token = lax.broadcasted_iota(jnp.int32, (tile, tokens), 0)
    out_token = lax.broadcasted_iota(jnp.int32, (tokens, width), 0)

    def score(r, count, slot):
        column_start = pl.multiple_of(lax.rem(r, heads) * width, width)
        all_keys = jnp.concatenate([prefix[:, pl.ds(column_start, width)], keys[r]], axis=0)
        q = queries[rows_of(r, group), :count, :].reshape(group * count, width)
        score_slots[slot][: group * count] = lax.dot_general(
            q, all_keys, (((1,), (1,)), ((), ())), preferred_element_type=jnp.float32
        )

    def weigh(count, slot):
        for start in range(0, group * count, tile):
            s = score_slots[slot][start : start + tile]
            own = jnp.where(column <= token + start % count, s[:, prefix_rows:], -jnp.inf)
            s = jnp.concatenate([s[:, :prefix_rows], own], axis=1)
            highest = jnp.max(s, axis=-1, keepdims=True)
            weights = jnp.exp2((s - highest) * exp2_scale)
            weight_slots[slot][start : start + tile] = weights.astype(jnp.bfloat16)

    def gather_values(r, count, length, slot):
        column_start = pl.multiple_of(value_base + lax.rem(r, heads) * width, width)
        all_values = jnp.concatenate([prefix[:, pl.ds(column_start, width)], values[r]], axis=0)
        all_values = jnp.concatenate([all_values, jnp.ones_like(all_values)], axis=1)
        summed = jnp.dot(
            weight_slots[slot][: group * count], all_values, preferred_element_type=jnp.float32
        )
        attended = (summed[:, :width] / summed[:, width:]).astype(jnp.bfloat16)
        attended = attended.reshape(group, count, width)
        span = rows_of(r, group)
        visible = (out_token[:count] < length)[None]
        staged[span, :count, :] = jnp.where(visible, attended, jnp.zeros_like(attended))
        if count < tokens:
            staged[span, count:, :] = jnp.zeros((group, tokens - count, width), jnp.bfloat16)
        pltpu.make_async_copy(staged.at[span], out.at[span], sems.at[r]).start()

    def block_of_rows(base, count, length):
        score(base, count, 0)
        for u in range(block):
            slot = u % 2
            if u + 1 < block:
                score(base + u + 1, count, 1 - slot)
            weigh(count, slot)
            gather_values(base + u, count, length, slot)

    def one_block(index, carry):
        base = index * block
        length = live[lax.div(place * rows + base, KEY_VALUE_HEADS)]
        tiles = jnp.clip(lax.div(length + tile - 1, tile), 1, tokens // tile)
        for n in range(1, tokens // tile + 1):
            pl.when(tiles == n)(functools.partial(block_of_rows, base, n * tile, length))
        return carry

    lax.fori_loop(0, rows // block, one_block, 0)

    def finish(r, carry):
        span = rows_of(r, group)
        pltpu.make_async_copy(staged.at[span], out.at[span], sems.at[r]).wait()
        return carry

    lax.fori_loop(0, rows, finish, 0)


def attend(lengths, queries, keys, values, prefix, heads):
    rows, tokens, _ = keys.shape
    group = queries.shape[0] // rows
    in_vmem = pl.BlockSpec(memory_space=pltpu.VMEM)
    in_smem = pl.BlockSpec(memory_space=pltpu.SMEM)
    wide = (group * tokens, prefix.shape[0] + tokens)
    return pl.pallas_call(
        functools.partial(
            attend_kernel,
            heads=heads,
            block=math.gcd(rows, KEY_VALUE_HEADS),
            tile=math.gcd(tokens, 32),
        ),
        out_shape=jax.ShapeDtypeStruct(queries.shape, jnp.bfloat16),
        in_specs=[in_smem] + [in_vmem] * 4,
        out_specs=pl.BlockSpec(memory_space=pl.ANY),
        scratch_shapes=[pltpu.VMEM(queries.shape, jnp.bfloat16)]
        + [pltpu.VMEM(wide, jnp.float32)] * 2
        + [pltpu.VMEM(wide, jnp.bfloat16)] * 2
        + [pltpu.SemaphoreType.DMA((rows,))],
        compiler_params=pltpu.CompilerParams(vmem_limit_bytes=36 << 20),
        name="attend",
    )(lengths, queries, keys, values, prefix)


def shards(
    cand_queries,
    candidate_keys,
    candidate_values,
    prefix_rotated_keys,
    prefix_value_matrix,
    lengths,
):
    sequence_count = lax.axis_size("seq")
    grp_count = lax.axis_size("grp")
    key_value_rows, cand_length, _ = candidate_keys.shape
    heads = min(KEY_VALUE_HEADS, key_value_rows)
    prefix_total = prefix_rotated_keys.shape[0] * sequence_count * grp_count
    wanted = (
        np.arange(sequence_count)[:, None] * key_value_rows + np.arange(heads)[None, :]
    ) % KEY_VALUE_HEADS

    def by_target(matrix):
        split = matrix.reshape(matrix.shape[0], KEY_VALUE_HEADS, HEAD_WIDTH)
        picked = jnp.take(split, wanted.reshape(-1), axis=1)
        return picked.reshape(matrix.shape[0], sequence_count, heads * HEAD_WIDTH).transpose(1, 0, 2)

    near_seq = math.gcd(sequence_count, 2)
    near_grp = math.gcd(grp_count, 2)
    far_seq, far_grp = sequence_count // near_seq, grp_count // near_grp

    def moved(block, far_g, near_g, far_s, near_s):
        if not (far_g or near_g or far_s or near_s):
            return block
        pairs = []
        for source in range(grp_count * sequence_count):
            g, s = divmod(source, sequence_count)
            g = (g // near_grp + far_g) % far_grp * near_grp + (g + near_g) % near_grp
            s = (s // near_seq + far_s) % far_seq * near_seq + (s + near_s) % near_seq
            pairs.append((source, g * sequence_count + s))
        return lax.ppermute(block, ("grp", "seq"), pairs)

    cosine, sine = rotation_tables(prefix_total, cand_length)
    queries, keys = rotated(cosine, sine, cand_queries, candidate_keys)
    if key_value_rows % KEY_VALUE_HEADS == 0:
        spare = prefix_rotated_keys.shape[1]
        zero = jnp.zeros((), jnp.bfloat16)
        block = lax.pad(prefix_rotated_keys, zero, ((0, 0, 0), (0, spare, 0))) + lax.pad(
            prefix_value_matrix, zero, ((0, 0, 0), (spare, 0, 0))
        )
        block = jnp.concatenate([moved(block, 0, 0, d, 0) for d in range(far_seq)], axis=0)
        block, queries, keys = lax.optimization_barrier((block, queries, keys))
        block = jnp.concatenate(
            [moved(block, e, 0, 0, d) for e in range(far_grp) for d in range(near_seq)], axis=0
        )
        prefix = jnp.concatenate([moved(block, 0, e, 0, 0) for e in range(near_grp)], axis=0)
    else:
        outgoing = jnp.concatenate(
            [by_target(prefix_rotated_keys), by_target(prefix_value_matrix)], axis=2
        )
        spread = lax.all_to_all(outgoing, "seq", split_axis=0, concat_axis=0, tiled=True)
        spread = spread.reshape(-1, 2 * heads * HEAD_WIDTH)
        prefix = lax.all_gather(spread, "grp", axis=0, tiled=True)
    values = candidate_values
    return attend(lengths, queries, keys, values, prefix, heads)


def solution(mesh):
    return jax.shard_map(
        shards,
        mesh=mesh,
        in_specs=(
            P(("grp", "seq"), None, None),
            P(("grp", "seq"), None, None),
            P(("grp", "seq"), None, None),
            P(("grp", "seq"), None),
            P(("grp", "seq"), None),
            P(),
        ),
        out_specs=P(("grp", "seq"), None, None),
        check_vma=False,
    )
```

```python
import functools
import math

import jax
import jax.numpy as jnp
import numpy as np
from jax import lax
from jax.experimental import pallas as pl
from jax.experimental.pallas import tpu as pltpu
from jax.sharding import PartitionSpec as P

QUERY_HEADS = 64
KEY_VALUE_HEADS = 8
HEAD_WIDTH = 128

rope_base = 500000.0
exp2_scale = math.log2(math.e) / math.sqrt(HEAD_WIDTH)
overflow_margin = 64.0
prepare_vmem = (47_000_000, 38_000_000)
attend_vmem = 20_000_000


def rotation_tables(first, count):
    half_width = HEAD_WIDTH // 2
    exponents = jnp.arange(half_width, dtype=jnp.float32) * (2.0 / HEAD_WIDTH)
    frequency = 1.0 / jnp.power(jnp.float32(rope_base), exponents)
    positions = (first + jnp.arange(count, dtype=jnp.int32)).astype(jnp.float32)
    angles = positions[:, None] * frequency[None, :]
    cosine = jnp.cos(angles)
    sine = jnp.sin(angles)
    return jnp.concatenate([cosine, cosine], axis=1), jnp.concatenate([-sine, sine], axis=1)


def rows_of(index, count):
    return pl.ds(pl.multiple_of(index * count, count), count)


def prepare_kernel(
    cosine,
    sine,
    queries,
    keys,
    out_q,
    out_k,
    out_w,
    out_m,
    raw_q,
    raw_k,
    scores_a,
    scores_b,
    q_sems,
    key_sem,
    *,
    first,
    tile,
):
    rows, tokens, width = raw_k.shape
    group = raw_q.shape[0] // rows
    score_slots = (scores_a, scores_b)
    column = lax.broadcasted_iota(jnp.int32, (tile, tokens), 1)
    token = lax.broadcasted_iota(jnp.int32, (tile, tokens), 0)

    def load(r):
        here = rows_of(r, group)
        there = pl.ds(pl.multiple_of((first + r) * group, group), group)
        return pltpu.make_async_copy(queries.at[there], raw_q.at[here], q_sems.at[r])

    keys_in = pltpu.make_async_copy(keys.at[pl.ds(first, rows)], raw_k, key_sem)
    keys_in.start()

    def start(r, carry):
        load(r).start()
        return carry

    lax.fori_loop(0, rows, start, 0)

    def rotate(x):
        x = x.astype(jnp.float32)
        turned = pltpu.roll(x, width // 2, x.ndim - 1)
        return (x * cosine[...] + turned * sine[...]).astype(jnp.bfloat16)

    def score(r, slot):
        load(r).wait()
        span = rows_of(r, group)
        q = rotate(raw_q[span])
        k = rotate(raw_k[r])
        out_q[span] = q
        out_k[r] = k
        score_slots[slot][...] = lax.dot_general(
            q.reshape(group * tokens, width),
            k,
            (((1,), (1,)), ((), ())),
            preferred_element_type=jnp.float32,
        )

    def weigh(r, slot):
        for h in range(group):
            for t in range(0, tokens, tile):
                begin = h * tokens + t
                s = score_slots[slot][begin : begin + tile]
                s = jnp.where(column <= token + t, s, -jnp.inf)
                highest = jnp.max(s, axis=-1, keepdims=True)
                weights = jnp.exp2((s - highest) * exp2_scale)
                out_w[r * group + h, t : t + tile, :] = weights.astype(jnp.bfloat16)
                out_m[r * group + h, t : t + tile, :] = jnp.broadcast_to(highest, (tile, width))

    keys_in.wait()
    score(0, 0)

    def two_rows(step, carry):
        for u in range(2):
            r = step * 2 + u
            score(r + 1, 1 - u)
            weigh(r, u)
        return carry

    pairs = (rows - 1) // 2
    lax.fori_loop(0, pairs, two_rows, 0)
    for r in range(2 * pairs, rows):
        if r + 1 < rows:
            score(r + 1, (r + 1) % 2)
        weigh(r, r % 2)


def prepare(cosine, sine, queries, keys, first, rows, vmem):
    total, tokens, width = keys.shape
    group = queries.shape[0] // total
    in_vmem = pl.BlockSpec(memory_space=pltpu.VMEM)
    in_hbm = pl.BlockSpec(memory_space=pltpu.HBM)
    return pl.pallas_call(
        functools.partial(prepare_kernel, first=first, tile=math.gcd(tokens, 64)),
        out_shape=[
            jax.ShapeDtypeStruct((rows * group, tokens, width), jnp.bfloat16),
            jax.ShapeDtypeStruct((rows, tokens, width), jnp.bfloat16),
            jax.ShapeDtypeStruct((rows * group, tokens, tokens), jnp.bfloat16),
            jax.ShapeDtypeStruct((rows * group, tokens, width), jnp.float32),
        ],
        in_specs=[in_vmem] * 2 + [in_hbm] * 2,
        out_specs=[in_vmem] * 4,
        scratch_shapes=[
            pltpu.VMEM((rows * group, tokens, width), jnp.bfloat16),
            pltpu.VMEM((rows, tokens, width), jnp.bfloat16),
            pltpu.VMEM((group * tokens, tokens), jnp.float32),
            pltpu.VMEM((group * tokens, tokens), jnp.float32),
            pltpu.SemaphoreType.DMA((rows,)),
            pltpu.SemaphoreType.DMA(()),
        ],
        cost_estimate=pl.CostEstimate(
            flops=2 * rows * group * tokens * tokens * width,
            bytes_accessed=2 * rows * (group + 1) * tokens * width,
            transcendentals=rows * group * tokens * tokens,
        ),
        compiler_params=pltpu.CompilerParams(vmem_limit_bytes=vmem),
        name="prepare",
    )(cosine, sine, queries, keys)


def attend_kernel(live, values, prefix, *refs, parts, heads, block, tile):
    prepared = [refs[4 * p : 4 * p + 4] for p in range(parts)]
    out, staged, score_a, score_b, weight_a, weight_b, guard, sems = refs[4 * parts :]
    score_slots, weight_slots = (score_a, score_b), (weight_a, weight_b)
    rows, tokens, width = values.shape
    group = out.shape[0] // rows
    part_rows = rows // parts
    prefix_rows = prefix.shape[0]
    value_base = heads * width
    place = lax.axis_index("grp") * lax.axis_size("seq") + lax.axis_index("seq")
    column = lax.broadcasted_iota(jnp.int32, (tile, tokens), 1)
    token = lax.broadcasted_iota(jnp.int32, (tile, tokens), 0)
    out_token = lax.broadcasted_iota(jnp.int32, (tokens, width), 0)
    guard[...] = jnp.full(guard.shape, -jnp.inf, jnp.float32)

    def prefix_keys(r):
        return prefix[:, pl.ds(pl.multiple_of(lax.rem(r, heads) * width, width), width)]

    def score(part, r, count, slot, own_too):
        queries, keys = prepared[part][0], prepared[part][1]
        here = r - part * part_rows
        q = queries[rows_of(here, group), :count, :].reshape(group * count, width)
        k = prefix_keys(r)
        if own_too:
            k = jnp.concatenate([k, keys[here]], axis=0)
        score_slots[slot][: group * count, : k.shape[0]] = lax.dot_general(
            q, k, (((1,), (1,)), ((), ())), preferred_element_type=jnp.float32
        )

    def across(x):
        if prefix_rows % width:
            return x[:, :1]
        return jnp.concatenate([x] * (prefix_rows // width), axis=1)

    def weigh_prefix(part, r, count, slot):
        own_w, own_m = prepared[part][2], prepared[part][3]
        base = (r - part * part_rows) * group
        worst = jnp.full((8, prefix_rows), -jnp.inf, jnp.float32)
        for h in range(group):
            for t in range(0, count, tile):
                begin = h * count + t
                s = score_slots[slot][begin : begin + tile, :prefix_rows]
                above = (s - across(own_m[base + h, t : t + tile, :])) * exp2_scale
                worst = jnp.maximum(worst, jnp.max(above.reshape(-1, 8, prefix_rows), axis=0))
                weight_slots[slot][begin : begin + tile, :prefix_rows] = jnp.exp2(above).astype(
                    jnp.bfloat16
                )
        guard[...] = jnp.maximum(guard[...], worst)

    def weigh_all(count, slot):
        for begin in range(0, group * count, tile):
            s = score_slots[slot][begin : begin + tile]
            own = jnp.where(column <= token + begin % count, s[:, prefix_rows:], -jnp.inf)
            s = jnp.concatenate([s[:, :prefix_rows], own], axis=1)
            highest = jnp.max(s, axis=-1, keepdims=True)
            weights = jnp.exp2((s - highest) * exp2_scale)
            weight_slots[slot][begin : begin + tile] = weights.astype(jnp.bfloat16)

    def gather_values(part, r, count, length, slot, own_too):
        column_start = pl.multiple_of(value_base + lax.rem(r, heads) * width, width)
        all_values = jnp.concatenate([prefix[:, pl.ds(column_start, width)], values[r]], axis=0)
        all_values = jnp.concatenate([all_values, jnp.ones_like(all_values)], axis=1)
        if own_too:
            weights = weight_slots[slot][: group * count]
        else:
            own = prepared[part][2][rows_of(r - part * part_rows, group), :count, :]
            weights = jnp.concatenate(
                [
                    weight_slots[slot][: group * count, :prefix_rows],
                    own.reshape(group * count, tokens),
                ],
                axis=1,
            )
        summed = jnp.dot(weights, all_values, preferred_element_type=jnp.float32)
        attended = (summed[:, :width] / summed[:, width:]).astype(jnp.bfloat16)
        attended = attended.reshape(group, count, width)
        span = rows_of(r, group)
        visible = (out_token[:count] < length)[None]
        staged[span, :count, :] = jnp.where(visible, attended, jnp.zeros_like(attended))
        if count < tokens:
            staged[span, count:, :] = jnp.zeros((group, tokens - count, width), jnp.bfloat16)
        pltpu.make_async_copy(staged.at[span], out.at[span], sems.at[r]).start()

    def length_of(r):
        return live[lax.div(place * rows + r, KEY_VALUE_HEADS)]

    def block_of_rows(part, base, count, length):
        score(part, base, count, 0, False)
        for u in range(block):
            slot = u % 2
            if u + 1 < block:
                score(part, base + u + 1, count, 1 - slot, False)
            weigh_prefix(part, base + u, count, slot)
            gather_values(part, base + u, count, length, slot, False)

    for part in range(parts):

        def one_block(index, carry, part=part):
            base = part * part_rows + index * block
            length = length_of(base)
            tiles = jnp.clip(lax.div(length + tile - 1, tile), 1, tokens // tile)
            for n in range(1, tokens // tile + 1):
                run = functools.partial(block_of_rows, part, base, n * tile, length)
                pl.when(tiles == n)(run)
            return carry

        lax.fori_loop(0, part_rows // block, one_block, 0)

    def finish(r, carry):
        span = rows_of(r, group)
        pltpu.make_async_copy(staged.at[span], out.at[span], sems.at[r]).wait()
        return carry

    lax.fori_loop(0, rows, finish, 0)

    @pl.when(jnp.max(guard[...]) > overflow_margin)
    def _():
        for part in range(parts):

            def one_row(index, carry, part=part):
                r = part * part_rows + index
                score(part, r, tokens, 0, True)
                weigh_all(tokens, 0)
                gather_values(part, r, tokens, length_of(r), 0, True)
                return carry

            lax.fori_loop(0, part_rows, one_row, 0)
        lax.fori_loop(0, rows, finish, 0)


def attend(lengths, values, prefix, prepared, rows_out, heads):
    rows, tokens, width = values.shape
    group = rows_out // rows
    parts = len(prepared)
    in_vmem = pl.BlockSpec(memory_space=pltpu.VMEM)
    in_smem = pl.BlockSpec(memory_space=pltpu.SMEM)
    wide = (group * tokens, prefix.shape[0] + tokens)
    return pl.pallas_call(
        functools.partial(
            attend_kernel,
            parts=parts,
            heads=heads,
            block=math.gcd(rows // parts, KEY_VALUE_HEADS),
            tile=math.gcd(tokens, 32),
        ),
        out_shape=jax.ShapeDtypeStruct((rows_out, tokens, width), jnp.bfloat16),
        in_specs=[in_smem] + [in_vmem] * (2 + 4 * parts),
        out_specs=pl.BlockSpec(memory_space=pl.ANY),
        scratch_shapes=[pltpu.VMEM((rows_out, tokens, width), jnp.bfloat16)]
        + [pltpu.VMEM(wide, jnp.float32)] * 2
        + [pltpu.VMEM(wide, jnp.bfloat16)] * 2
        + [pltpu.VMEM((8, prefix.shape[0]), jnp.float32), pltpu.SemaphoreType.DMA((rows,))],
        compiler_params=pltpu.CompilerParams(vmem_limit_bytes=attend_vmem),
        name="attend",
    )(lengths, values, prefix, *[x for part in prepared for x in part])


def shards(
    cand_queries,
    candidate_keys,
    candidate_values,
    prefix_rotated_keys,
    prefix_value_matrix,
    lengths,
):
    sequence_count = lax.axis_size("seq")
    grp_count = lax.axis_size("grp")
    key_value_rows, cand_length, _ = candidate_keys.shape
    heads = min(KEY_VALUE_HEADS, key_value_rows)
    prefix_total = prefix_rotated_keys.shape[0] * sequence_count * grp_count
    wanted = (
        np.arange(sequence_count)[:, None] * key_value_rows + np.arange(heads)[None, :]
    ) % KEY_VALUE_HEADS

    def by_target(matrix):
        split = matrix.reshape(matrix.shape[0], KEY_VALUE_HEADS, HEAD_WIDTH)
        picked = jnp.take(split, wanted.reshape(-1), axis=1)
        return picked.reshape(matrix.shape[0], sequence_count, heads * HEAD_WIDTH).transpose(1, 0, 2)

    near_seq = math.gcd(sequence_count, 2)
    near_grp = math.gcd(grp_count, 2)
    far_seq, far_grp = sequence_count // near_seq, grp_count // near_grp

    def moved(block, far_g, near_g, far_s, near_s):
        if not (far_g or near_g or far_s or near_s):
            return block
        pairs = []
        for source in range(grp_count * sequence_count):
            g, s = divmod(source, sequence_count)
            g = (g // near_grp + far_g) % far_grp * near_grp + (g + near_g) % near_grp
            s = (s // near_seq + far_s) % far_seq * near_seq + (s + near_s) % near_seq
            pairs.append((source, g * sequence_count + s))
        return lax.ppermute(block, ("grp", "seq"), pairs)

    cosine, sine = rotation_tables(prefix_total, cand_length)
    parts = math.gcd(key_value_rows, 2)
    part_rows = key_value_rows // parts

    def prepared_part(p, cosine, sine):
        return prepare(
            cosine, sine, cand_queries, candidate_keys, p * part_rows, part_rows, prepare_vmem[p]
        )

    prepared = [prepared_part(0, cosine, sine)]
    if key_value_rows % KEY_VALUE_HEADS == 0:
        spare = prefix_rotated_keys.shape[1]
        zero = jnp.zeros((), jnp.bfloat16)
        block = lax.pad(prefix_rotated_keys, zero, ((0, 0, 0), (0, spare, 0))) + lax.pad(
            prefix_value_matrix, zero, ((0, 0, 0), (spare, 0, 0))
        )
        block = jnp.concatenate([moved(block, 0, 0, d, 0) for d in range(far_seq)], axis=0)
        block, prepared, cosine, sine = lax.optimization_barrier((block, prepared, cosine, sine))
        block = jnp.concatenate(
            [moved(block, e, 0, 0, d) for e in range(far_grp) for d in range(near_seq)], axis=0
        )
        prepared += [prepared_part(p, cosine, sine) for p in range(1, parts)]
        block, prepared = lax.optimization_barrier((block, prepared))
        prefix = jnp.concatenate([moved(block, 0, e, 0, 0) for e in range(near_grp)], axis=0)
    else:
        outgoing = jnp.concatenate(
            [by_target(prefix_rotated_keys), by_target(prefix_value_matrix)], axis=2
        )
        spread = lax.all_to_all(outgoing, "seq", split_axis=0, concat_axis=0, tiled=True)
        spread = spread.reshape(-1, 2 * heads * HEAD_WIDTH)
        prefix = lax.all_gather(spread, "grp", axis=0, tiled=True)
        prepared += [prepared_part(p, cosine, sine) for p in range(1, parts)]
    return attend(lengths, candidate_values, prefix, prepared, cand_queries.shape[0], heads)


def solution(mesh):
    return jax.shard_map(
        shards,
        mesh=mesh,
        in_specs=(
            P(("grp", "seq"), None, None),
            P(("grp", "seq"), None, None),
            P(("grp", "seq"), None, None),
            P(("grp", "seq"), None),
            P(("grp", "seq"), None),
            P(),
        ),
        out_specs=P(("grp", "seq"), None, None),
        check_vma=False,
    )
```

```python
import functools
import math

import jax
import jax.numpy as jnp
import numpy as np
from jax import lax
from jax.experimental import pallas as pl
from jax.experimental.pallas import tpu as pltpu
from jax.sharding import PartitionSpec as P

QUERY_HEADS = 64
KEY_VALUE_HEADS = 8
HEAD_WIDTH = 128

rope_base = 500000.0
exp2_scale = math.log2(math.e) / math.sqrt(HEAD_WIDTH)
overflow_margin = 64.0
prepare_vmem = (47_000_000, 38_000_000)
attend_vmem = 20_000_000


def rotation_tables(first, count):
    half_width = HEAD_WIDTH // 2
    exponents = jnp.arange(half_width, dtype=jnp.float32) * (2.0 / HEAD_WIDTH)
    frequency = 1.0 / jnp.power(jnp.float32(rope_base), exponents)
    positions = (first + jnp.arange(count, dtype=jnp.int32)).astype(jnp.float32)
    angles = positions[:, None] * frequency[None, :]
    cosine = jnp.cos(angles)
    sine = jnp.sin(angles)
    return jnp.concatenate([cosine, cosine], axis=1), jnp.concatenate([-sine, sine], axis=1)


def rows_of(index, count):
    return pl.ds(pl.multiple_of(index * count, count), count)


def prepare_kernel(
    cosine,
    sine,
    queries,
    keys,
    out_q,
    out_k,
    out_w,
    out_m,
    raw_q,
    raw_k,
    scores_a,
    scores_b,
    q_sems,
    key_sem,
    *,
    first,
    tile,
):
    rows, tokens, width = raw_k.shape
    group = raw_q.shape[0] // rows
    score_slots = (scores_a, scores_b)
    column = lax.broadcasted_iota(jnp.int32, (tile, tokens), 1)
    token = lax.broadcasted_iota(jnp.int32, (tile, tokens), 0)

    def load(r):
        here = rows_of(r, group)
        there = pl.ds(pl.multiple_of((first + r) * group, group), group)
        return pltpu.make_async_copy(queries.at[there], raw_q.at[here], q_sems.at[r])

    keys_in = pltpu.make_async_copy(keys.at[pl.ds(first, rows)], raw_k, key_sem)
    keys_in.start()

    def start(r, carry):
        load(r).start()
        return carry

    lax.fori_loop(0, rows, start, 0)

    def rotate(x):
        x = x.astype(jnp.float32)
        turned = pltpu.roll(x, width // 2, x.ndim - 1)
        return (x * cosine[...] + turned * sine[...]).astype(jnp.bfloat16)

    def score(r, slot):
        load(r).wait()
        span = rows_of(r, group)
        q = rotate(raw_q[span])
        k = rotate(raw_k[r])
        out_q[span] = q
        out_k[r] = k
        score_slots[slot][...] = lax.dot_general(
            q.reshape(group * tokens, width),
            k,
            (((1,), (1,)), ((), ())),
            preferred_element_type=jnp.float32,
        )

    def weigh(r, slot):
        for h in range(group):
            for t in range(0, tokens, tile):
                begin = h * tokens + t
                s = score_slots[slot][begin : begin + tile]
                s = jnp.where(column <= token + t, s, -jnp.inf)
                highest = jnp.max(s, axis=-1, keepdims=True)
                weights = jnp.exp2((s - highest) * exp2_scale)
                out_w[r * group + h, t : t + tile, :] = weights.astype(jnp.bfloat16)
                out_m[r * group + h, t : t + tile, :] = jnp.broadcast_to(highest, (tile, width))

    keys_in.wait()
    score(0, 0)

    def two_rows(step, carry):
        for u in range(2):
            r = step * 2 + u
            score(r + 1, 1 - u)
            weigh(r, u)
        return carry

    pairs = (rows - 1) // 2
    lax.fori_loop(0, pairs, two_rows, 0)
    for r in range(2 * pairs, rows):
        if r + 1 < rows:
            score(r + 1, (r + 1) % 2)
        weigh(r, r % 2)


def prepare(cosine, sine, queries, keys, first, rows, vmem):
    total, tokens, width = keys.shape
    group = queries.shape[0] // total
    in_vmem = pl.BlockSpec(memory_space=pltpu.VMEM)
    in_hbm = pl.BlockSpec(memory_space=pltpu.HBM)
    return pl.pallas_call(
        functools.partial(prepare_kernel, first=first, tile=math.gcd(tokens, 128)),
        out_shape=[
            jax.ShapeDtypeStruct((rows * group, tokens, width), jnp.bfloat16),
            jax.ShapeDtypeStruct((rows, tokens, width), jnp.bfloat16),
            jax.ShapeDtypeStruct((rows * group, tokens, tokens), jnp.bfloat16),
            jax.ShapeDtypeStruct((rows * group, tokens, width), jnp.float32),
        ],
        in_specs=[in_vmem] * 2 + [in_hbm] * 2,
        out_specs=[in_vmem] * 4,
        scratch_shapes=[
            pltpu.VMEM((rows * group, tokens, width), jnp.bfloat16),
            pltpu.VMEM((rows, tokens, width), jnp.bfloat16),
            pltpu.VMEM((group * tokens, tokens), jnp.float32),
            pltpu.VMEM((group * tokens, tokens), jnp.float32),
            pltpu.SemaphoreType.DMA((rows,)),
            pltpu.SemaphoreType.DMA(()),
        ],
        cost_estimate=pl.CostEstimate(
            flops=2 * rows * group * tokens * tokens * width,
            bytes_accessed=2 * rows * (group + 1) * tokens * width,
            transcendentals=rows * group * tokens * tokens,
        ),
        compiler_params=pltpu.CompilerParams(vmem_limit_bytes=vmem),
        name="prepare",
    )(cosine, sine, queries, keys)


def attend_kernel(live, values, prefix, *refs, parts, heads, block, tile):
    prepared = [refs[4 * p : 4 * p + 4] for p in range(parts)]
    out, staged, score_a, score_b, weight_a, weight_b, guard, sems = refs[4 * parts :]
    score_slots, weight_slots = (score_a, score_b), (weight_a, weight_b)
    rows, tokens, width = values.shape
    group = out.shape[0] // rows
    part_rows = rows // parts
    prefix_rows = prefix.shape[0]
    value_base = heads * width
    place = lax.axis_index("grp") * lax.axis_size("seq") + lax.axis_index("seq")
    column = lax.broadcasted_iota(jnp.int32, (tile, tokens), 1)
    token = lax.broadcasted_iota(jnp.int32, (tile, tokens), 0)
    out_token = lax.broadcasted_iota(jnp.int32, (tokens, width), 0)
    guard[...] = jnp.full(guard.shape, -jnp.inf, jnp.float32)

    def prefix_keys(r):
        return prefix[:, pl.ds(pl.multiple_of(lax.rem(r, heads) * width, width), width)]

    def score(part, r, count, slot, own_too):
        queries, keys = prepared[part][0], prepared[part][1]
        here = r - part * part_rows
        q = queries[rows_of(here, group), :count, :].reshape(group * count, width)
        k = prefix_keys(r)
        if own_too:
            k = jnp.concatenate([k, keys[here]], axis=0)
        score_slots[slot][: group * count, : k.shape[0]] = lax.dot_general(
            q, k, (((1,), (1,)), ((), ())), preferred_element_type=jnp.float32
        )

    def across(x):
        if prefix_rows % width:
            return x[:, :1]
        return jnp.concatenate([x] * (prefix_rows // width), axis=1)

    def weigh_prefix(part, r, count, slot):
        own_w, own_m = prepared[part][2], prepared[part][3]
        base = (r - part * part_rows) * group
        worst = jnp.full((8, prefix_rows), -jnp.inf, jnp.float32)
        for h in range(group):
            for t in range(0, count, tile):
                begin = h * count + t
                s = score_slots[slot][begin : begin + tile, :prefix_rows]
                above = (s - across(own_m[base + h, t : t + tile, :])) * exp2_scale
                worst = jnp.maximum(worst, jnp.max(above.reshape(-1, 8, prefix_rows), axis=0))
                weight_slots[slot][begin : begin + tile, :prefix_rows] = jnp.exp2(above).astype(
                    jnp.bfloat16
                )
        guard[...] = jnp.maximum(guard[...], worst)

    def weigh_all(count, slot):
        for begin in range(0, group * count, tile):
            s = score_slots[slot][begin : begin + tile]
            own = jnp.where(column <= token + begin % count, s[:, prefix_rows:], -jnp.inf)
            s = jnp.concatenate([s[:, :prefix_rows], own], axis=1)
            highest = jnp.max(s, axis=-1, keepdims=True)
            weights = jnp.exp2((s - highest) * exp2_scale)
            weight_slots[slot][begin : begin + tile] = weights.astype(jnp.bfloat16)

    def gather_values(part, r, count, length, slot, own_too):
        column_start = pl.multiple_of(value_base + lax.rem(r, heads) * width, width)
        all_values = jnp.concatenate([prefix[:, pl.ds(column_start, width)], values[r]], axis=0)
        all_values = jnp.concatenate([all_values, jnp.ones_like(all_values)], axis=1)
        if own_too:
            weights = weight_slots[slot][: group * count]
        else:
            own = prepared[part][2][rows_of(r - part * part_rows, group), :count, :]
            weights = jnp.concatenate(
                [
                    weight_slots[slot][: group * count, :prefix_rows],
                    own.reshape(group * count, tokens),
                ],
                axis=1,
            )
        summed = jnp.dot(weights, all_values, preferred_element_type=jnp.float32)
        attended = (summed[:, :width] / summed[:, width:]).astype(jnp.bfloat16)
        attended = attended.reshape(group, count, width)
        span = rows_of(r, group)
        visible = (out_token[:count] < length)[None]
        staged[span, :count, :] = jnp.where(visible, attended, jnp.zeros_like(attended))
        if count < tokens:
            staged[span, count:, :] = jnp.zeros((group, tokens - count, width), jnp.bfloat16)
        pltpu.make_async_copy(staged.at[span], out.at[span], sems.at[r]).start()

    def length_of(r):
        return live[lax.div(place * rows + r, KEY_VALUE_HEADS)]

    def block_of_rows(part, base, count, length):
        score(part, base, count, 0, False)
        for u in range(block):
            slot = u % 2
            if u + 1 < block:
                score(part, base + u + 1, count, 1 - slot, False)
            weigh_prefix(part, base + u, count, slot)
            gather_values(part, base + u, count, length, slot, False)

    for part in range(parts):

        def one_block(index, carry, part=part):
            base = part * part_rows + index * block
            length = length_of(base)
            tiles = jnp.clip(lax.div(length + tile - 1, tile), 1, tokens // tile)
            for n in range(1, tokens // tile + 1):
                run = functools.partial(block_of_rows, part, base, n * tile, length)
                pl.when(tiles == n)(run)
            return carry

        lax.fori_loop(0, part_rows // block, one_block, 0)

    def finish(r, carry):
        span = rows_of(r, group)
        pltpu.make_async_copy(staged.at[span], out.at[span], sems.at[r]).wait()
        return carry

    lax.fori_loop(0, rows, finish, 0)

    @pl.when(jnp.max(guard[...]) > overflow_margin)
    def _():
        for part in range(parts):

            def one_row(index, carry, part=part):
                r = part * part_rows + index
                score(part, r, tokens, 0, True)
                weigh_all(tokens, 0)
                gather_values(part, r, tokens, length_of(r), 0, True)
                return carry

            lax.fori_loop(0, part_rows, one_row, 0)
        lax.fori_loop(0, rows, finish, 0)


def attend(lengths, values, prefix, prepared, rows_out, heads):
    rows, tokens, width = values.shape
    group = rows_out // rows
    parts = len(prepared)
    in_vmem = pl.BlockSpec(memory_space=pltpu.VMEM)
    in_smem = pl.BlockSpec(memory_space=pltpu.SMEM)
    wide = (group * tokens, prefix.shape[0] + tokens)
    return pl.pallas_call(
        functools.partial(
            attend_kernel,
            parts=parts,
            heads=heads,
            block=math.gcd(rows // parts, KEY_VALUE_HEADS),
            tile=math.gcd(tokens, 32),
        ),
        out_shape=jax.ShapeDtypeStruct((rows_out, tokens, width), jnp.bfloat16),
        in_specs=[in_smem] + [in_vmem] * (2 + 4 * parts),
        out_specs=pl.BlockSpec(memory_space=pl.ANY),
        scratch_shapes=[pltpu.VMEM((rows_out, tokens, width), jnp.bfloat16)]
        + [pltpu.VMEM(wide, jnp.float32)] * 2
        + [pltpu.VMEM(wide, jnp.bfloat16)] * 2
        + [pltpu.VMEM((8, prefix.shape[0]), jnp.float32), pltpu.SemaphoreType.DMA((rows,))],
        compiler_params=pltpu.CompilerParams(vmem_limit_bytes=attend_vmem),
        name="attend",
    )(lengths, values, prefix, *[x for part in prepared for x in part])


def shards(
    cand_queries,
    candidate_keys,
    candidate_values,
    prefix_rotated_keys,
    prefix_value_matrix,
    lengths,
):
    sequence_count = lax.axis_size("seq")
    grp_count = lax.axis_size("grp")
    key_value_rows, cand_length, _ = candidate_keys.shape
    heads = min(KEY_VALUE_HEADS, key_value_rows)
    prefix_total = prefix_rotated_keys.shape[0] * sequence_count * grp_count
    wanted = (
        np.arange(sequence_count)[:, None] * key_value_rows + np.arange(heads)[None, :]
    ) % KEY_VALUE_HEADS

    def by_target(matrix):
        split = matrix.reshape(matrix.shape[0], KEY_VALUE_HEADS, HEAD_WIDTH)
        picked = jnp.take(split, wanted.reshape(-1), axis=1)
        return picked.reshape(matrix.shape[0], sequence_count, heads * HEAD_WIDTH).transpose(1, 0, 2)

    near_seq = math.gcd(sequence_count, 2)
    near_grp = math.gcd(grp_count, 2)
    far_seq, far_grp = sequence_count // near_seq, grp_count // near_grp

    def moved(block, far_g, near_g, far_s, near_s):
        if not (far_g or near_g or far_s or near_s):
            return block
        pairs = []
        for source in range(grp_count * sequence_count):
            g, s = divmod(source, sequence_count)
            g = (g // near_grp + far_g) % far_grp * near_grp + (g + near_g) % near_grp
            s = (s // near_seq + far_s) % far_seq * near_seq + (s + near_s) % near_seq
            pairs.append((source, g * sequence_count + s))
        return lax.ppermute(block, ("grp", "seq"), pairs)

    cosine, sine = rotation_tables(prefix_total, cand_length)
    parts = math.gcd(key_value_rows, 2)
    part_rows = key_value_rows // parts

    def prepared_part(p, cosine, sine):
        return prepare(
            cosine, sine, cand_queries, candidate_keys, p * part_rows, part_rows, prepare_vmem[p]
        )

    prepared = [prepared_part(0, cosine, sine)]
    if key_value_rows % KEY_VALUE_HEADS == 0:
        spare = prefix_rotated_keys.shape[1]
        zero = jnp.zeros((), jnp.bfloat16)
        block = lax.pad(prefix_rotated_keys, zero, ((0, 0, 0), (0, spare, 0))) + lax.pad(
            prefix_value_matrix, zero, ((0, 0, 0), (spare, 0, 0))
        )
        block = jnp.concatenate([moved(block, 0, 0, d, 0) for d in range(far_seq)], axis=0)
        block, prepared, cosine, sine = lax.optimization_barrier((block, prepared, cosine, sine))
        block = jnp.concatenate(
            [moved(block, e, 0, 0, d) for e in range(far_grp) for d in range(near_seq)], axis=0
        )
        prepared += [prepared_part(p, cosine, sine) for p in range(1, parts)]
        block, prepared = lax.optimization_barrier((block, prepared))
        prefix = jnp.concatenate([moved(block, 0, e, 0, 0) for e in range(near_grp)], axis=0)
    else:
        outgoing = jnp.concatenate(
            [by_target(prefix_rotated_keys), by_target(prefix_value_matrix)], axis=2
        )
        spread = lax.all_to_all(outgoing, "seq", split_axis=0, concat_axis=0, tiled=True)
        spread = spread.reshape(-1, 2 * heads * HEAD_WIDTH)
        prefix = lax.all_gather(spread, "grp", axis=0, tiled=True)
        prepared += [prepared_part(p, cosine, sine) for p in range(1, parts)]
    return attend(lengths, candidate_values, prefix, prepared, cand_queries.shape[0], heads)


def solution(mesh):
    return jax.shard_map(
        shards,
        mesh=mesh,
        in_specs=(
            P(("grp", "seq"), None, None),
            P(("grp", "seq"), None, None),
            P(("grp", "seq"), None, None),
            P(("grp", "seq"), None),
            P(("grp", "seq"), None),
            P(),
        ),
        out_specs=P(("grp", "seq"), None, None),
        check_vma=False,
    )
```
